32 devices in a mesh: shot: 16 (over z, y, core), surf: 2 (over x).
Axes of the slice: x: 2, y: 2, z: 4, core: 2. Of those that a mesh axis runs over, the one named last changes fastest.
Arguments:
- data: float32 [32, 256, 512], P('shot', 'surf'), may hold values from -6 to 6
- positions: int32 [256], P('surf'), may hold values from 0 to 63, as said below
- plan: int32 [16], replicated, may hold values from 0 to 15, each once
- primaries: bfloat16 [64, 16, 16, 256], P('surf', None, 'shot'), may hold values from -0.03125 to 0.03125
- scale: float32 [32], P('shot'), may hold values from 0.5 to 1.5
Outputs:
- demultiplied: float32 [32, 256, 512], P('shot', 'surf')
The draws below stay inside these ranges and needn't reach their ends.
Inputs may be any that keep to these rules, and one draw needn't show every extreme that they name: `positions`: receiver r lies at a position of the block [b * 32, (b + 1) * 32) with b = r // 128; in each such block of receivers the first maps to the block's first position and the last to its last. A permutation: slot i of primaries holds receiver panel plan[i].
All inputs are finite; a program needn't handle non-finite values.
Results may differ from the reference program's by a relative error of at most 0.0065.
Values may be sent and summed in bfloat16 or wider, within the bound.
A program may use at most 128 MiB of HBM per device.

```python
import math
import jax
import jax.numpy as jnp
from jax import lax

S_DEV = 2
PD = 32
RP = 16
NT = 512
TAPS = 256
PANELS = 16
SHOTS = 32
RECV = 256
RECV_DEV = 128
POSITIONS = 64
N_SURF = 2


def draw_positions(key, part):
    receiver_index = jnp.arange(RECV, dtype=jnp.int32)
    offset = receiver_index % RECV_DEV
    block_index = receiver_index // RECV_DEV
    picked = jax.random.randint(key, (RECV,), 0, PD, dtype=jnp.int32)
    picked = jnp.where(offset == 0, 0, jnp.where(offset == RECV_DEV - 1, PD - 1, picked))
    return (block_index * PD + picked).astype(jnp.int32)


def levels(rng, shape, cuts, smallest, top_value):
    def one(axis_at, blocks):
        heights = jax.random.uniform(jax.random.fold_in(jax.random.fold_in(rng, 6), axis_at), (blocks,), jnp.float32, smallest / len(cuts), top_value / len(cuts))
        return jnp.repeat(jnp.exp(heights), shape[axis_at] // blocks).reshape((-1,) + (1,) * (len(shape) - axis_at - 1))

    gain = one(*cuts[0])
    for cut in cuts[1:]:
        gain = gain * one(*cut)
    return gain


def centred(rng, dims, width, limit, pieces=(), held_as=jnp.bfloat16):
    loudness = levels(rng, dims, pieces, -0.22, 0.18) if pieces else 1.0
    drawn = jax.random.normal(rng, dims, jnp.float32) * width * loudness
    return jnp.minimum(jnp.maximum(drawn, -limit), limit).astype(held_as)


def setup_inputs(seed: int = 0) -> dict:
    arg_keys = jax.random.split(jax.random.key(seed), 6)
    return {
        "data": centred(arg_keys[0], (SHOTS, RECV, NT), 1.0, 6.0, ((0, 16), (1, 2)), jnp.float32),
        "positions": draw_positions(jax.random.fold_in(arg_keys[5], 71), 0),
        "plan": jax.random.permutation(arg_keys[2], PANELS).astype(jnp.int32),
        "primaries": centred(arg_keys[3], (POSITIONS, RP, PANELS, TAPS), (2 * POSITIONS * TAPS) ** -0.5, 0.03125, ((0, 2), (2, 16))),
        "scale": jnp.clip(jnp.exp(math.log(1.5) - 1.0986123 * jax.random.uniform(arg_keys[4], (SHOTS,), jnp.float32) ** levels(arg_keys[4], (SHOTS,), ((0, 16),), -0.2, 0.2)), 0.5, 1.5),
    }


def fourier_matrices(samples):
    length = 2 * samples
    time_index = jnp.arange(samples, dtype=jnp.int32)
    phase_index = (time_index[:, None] * time_index[None, :]) % length
    angles = phase_index.astype(jnp.float32) * (2.0 * math.pi / length)
    cosine = jnp.cos(angles)
    sine_part = jnp.sin(angles)
    alternate = (1 - 2 * (time_index % 2)).astype(jnp.float32)
    nyquist = time_index == 0
    forward_imag = jnp.where(nyquist[None, :], alternate[:, None], -sine_part)
    forward = jnp.concatenate([cosine, forward_imag], axis=1).astype(jnp.bfloat16)
    weights = jnp.where(nyquist, 1.0, 2.0).astype(jnp.float32) / length
    backward_real_table = cosine.T * weights[:, None]
    inverse_imag = jnp.where(nyquist[:, None], alternate[None, :] / length, -2.0 * sine_part.T / length)
    inverse = jnp.concatenate([backward_real_table, inverse_imag], axis=0).astype(jnp.bfloat16)
    return forward, inverse


def spectral_product(left, right):
    half = left.shape[-1] // 2
    left_real = left[..., :half]
    left_imag = left[..., half:]
    right_real = right[..., :half]
    right_imag = right[..., half:]

    def contract(leading_factor, trailing_factor):
        return jnp.einsum("quw,ugw->qgw", leading_factor, trailing_factor, precision=lax.Precision.HIGHEST)

    real_cross_term = contract(left_real, right_real)
    imaginary_cross_term = contract(left_imag, right_imag)
    crossed = contract(left_real, right_imag) + contract(left_imag, right_real)
    interior = (jnp.arange(half) > 0).astype(jnp.float32)
    return jnp.concatenate([real_cross_term - interior * imaginary_cross_term, interior * crossed + (1.0 - interior) * imaginary_cross_term], axis=-1)


def reference(data, positions, plan, primaries, scale):
    shot_total, receiver_total, samples = data.shape
    position_total = primaries.shape[0]
    tap_count = primaries.shape[3]
    forward, inverse = fourier_matrices(samples)
    onehot = (positions[:, None] == jnp.arange(position_total, dtype=jnp.int32)[None, :]).astype(jnp.float32)
    gathered = jnp.einsum("srt,rx->sxt", data, onehot, precision=lax.Precision.HIGHEST).astype(jnp.bfloat16)
    data_spectra = jnp.dot(gathered.reshape(-1, samples), forward, preferred_element_type=jnp.float32)
    data_spectra = data_spectra.astype(jnp.bfloat16).reshape(shot_total, position_total, 2 * samples)
    panel_order = jnp.argsort(plan).astype(jnp.int32)
    arranged = jnp.take(primaries, panel_order, axis=2)
    primary_spectra = jnp.dot(arranged.reshape(-1, tap_count), forward[:tap_count], preferred_element_type=jnp.float32)
    primary_spectra = primary_spectra.astype(jnp.bfloat16).astype(jnp.float32).reshape(position_total, receiver_total, 2 * samples)

    def one_group(group_spectra):
        group_wide = group_spectra.astype(jnp.float32)
        running = jnp.zeros((group_spectra.shape[0], receiver_total, 2 * samples), jnp.float32)
        for block_index in range(N_SURF):
            low = block_index * PD
            term = spectral_product(group_wide[:, low:low + PD], primary_spectra[low:low + PD])
            rounded = lax.optimization_barrier(term.astype(jnp.bfloat16))
            running = running + rounded.astype(jnp.float32)
        spectrum = running.astype(jnp.bfloat16)
        in_time = jnp.dot(spectrum.reshape(-1, 2 * samples), inverse, preferred_element_type=jnp.float32)
        return in_time.reshape(group_spectra.shape[0], receiver_total, samples)

    grouped = data_spectra.reshape(shot_total // S_DEV, S_DEV, position_total, 2 * samples)
    prediction = lax.map(one_group, grouped).reshape(shot_total, receiver_total, samples)
    return data - scale[:, None, None] * prediction
```

```python
import functools
import math

import jax
import jax.numpy as jnp
import ml_dtypes
import numpy as np
from jax import lax
from jax.experimental import pallas as pl
from jax.experimental.pallas import tpu as pltpu
from jax.sharding import PartitionSpec as P

MESH = pl.DeviceIdType.MESH
F32 = jnp.float32
BF16 = jnp.bfloat16


def fourier_matrices(samples):
    length = 2 * samples
    index = np.arange(samples)
    angles = (index[:, None] * index[None, :] % length) * (2.0 * math.pi / length)
    cosine, sine = np.cos(angles), np.sin(angles)
    alternate = 1.0 - 2.0 * (index % 2)
    forward_imag = -sine
    forward_imag[:, 0] = alternate
    forward = np.concatenate([cosine, forward_imag], axis=1)
    weights = np.where(index == 0, 1.0, 2.0) / length
    weights = np.concatenate([weights, weights])
    inverse = forward.T * weights[:, None]
    return forward.astype(ml_dtypes.bfloat16), inverse.astype(ml_dtypes.bfloat16)


def chip_at(place, chips):
    half = chips // 2
    side = place // half
    return 2 * (place + side * (chips - 1 - 2 * place)) + side


def kernel(
    sizes,
    plan_ref, scale_ref, where_ref, positions_ref, data_ref, primaries_ref, forward_ref, inverse_ref,
    out_ref,
    gathered, partner, e1, e2, e3, dr, di, dsum, spectrum, leaving, arrived,
    panel_sems, ring_send, ring_recv, leave_send, leave_recv,
):
    chips, surfs, shots, depth, width, samples, taps = sizes
    per_surf = width // surfs
    panels = 2 * chips
    shot = lax.axis_index("shot")
    surf = lax.axis_index("surf")
    chip, core = shot // 2, shot % 2
    height, side = chip // 2, chip % 2
    place = height + side * (chips - 1 - 2 * height)
    right = chip_at((place + 1) % chips, chips) * 2 + core
    left = chip_at((place + chips - 1) % chips, chips) * 2 + core

    barrier = pltpu.get_barrier_semaphore()
    pl.semaphore_signal(barrier, inc=1, device_id=(chip * 2 + 1 - core, surf), device_id_type=MESH)

    def greet(n, carry):
        other = (n // surfs) * 2 + core
        to = n % surfs

        @pl.when(n != chip * surfs + surf)
        def _():
            pl.semaphore_signal(barrier, inc=1, device_id=(other, to), device_id_type=MESH)

        return carry

    lax.fori_loop(0, chips * surfs, greet, 0)

    local = positions_ref[...] - surf * depth
    onehot = jnp.where(
        lax.broadcasted_iota(jnp.int32, (depth, local.shape[1]), 0) == local, 1.0, 0.0
    ).astype(BF16)
    for s in range(shots):
        value = data_ref[s]
        top = value.astype(BF16)
        rest = value - top.astype(F32)
        middle = rest.astype(BF16)
        low = (rest - middle.astype(F32)).astype(BF16)
        total = (
            jnp.dot(onehot, top, preferred_element_type=F32)
            + jnp.dot(onehot, middle, preferred_element_type=F32)
            + jnp.dot(onehot, low, preferred_element_type=F32)
        )
        gathered[place, s * depth:(s + 1) * depth, :] = total.astype(BF16)

    pl.semaphore_wait(barrier, chips * surfs)

    def ring_copy(direction, hops):
        if direction == 0:
            slot, to = (place + chips - hops) % chips, right
        else:
            slot, to = (place + hops) % chips, left
        return pltpu.make_async_remote_copy(
            src_ref=gathered.at[slot],
            dst_ref=gathered.at[slot],
            send_sem=ring_send.at[direction, hops],
            recv_sem=ring_recv.at[slot],
            device_id=(to, surf),
            device_id_type=MESH,
        )

    right_hops, left_hops = chips // 2, (chips - 1) // 2
    ring_copy(0, 0).start()
    ring_copy(1, 0).start()
    panel_copy = pltpu.make_async_remote_copy(
        src_ref=primaries_ref,
        dst_ref=partner,
        send_sem=panel_sems.at[0],
        recv_sem=panel_sems.at[1],
        device_id=(chip * 2 + 1 - core, surf),
        device_id_type=MESH,
    )
    panel_copy.start()

    block = 8

    def panel_spectra(source, which):
        def step(n, carry):
            rows = source[pl.ds(pl.multiple_of(n * block * width, block * width), block * width), :]
            value = jnp.dot(rows, forward_ref[:taps, :], preferred_element_type=F32)
            real, imag = value[:, :samples], value[:, samples:]
            first = lax.broadcasted_iota(jnp.int32, real.shape, 1) == 0
            shape = (block, width, samples)
            at = pl.ds(n * block, block)
            e1[at, which] = jnp.where(first, 0.0, real).reshape(shape)
            e2[at, which] = jnp.where(first, real, imag - real).reshape(shape)
            e3[at, which] = jnp.where(first, imag, imag + real).reshape(shape)
            return carry

        lax.fori_loop(0, depth // block, step, 0)

    panel_spectra(primaries_ref, 0)
    panel_copy.wait_recv()
    panel_spectra(partner, 1)

    def leave_copy(slot, to):
        return pltpu.make_async_remote_copy(
            src_ref=leaving.at[slot, to],
            dst_ref=arrived.at[place, surf],
            send_sem=leave_send.at[slot, to],
            recv_sem=leave_recv.at[place, surf],
            device_id=(chip_at(slot, chips) * 2 + core, to),
            device_id_type=MESH,
        )

    def one_chunk(e, carry):
        hops = (e + 1) // 2

        @pl.when(e % 2 == 1)
        def _():
            pltpu.make_async_copy(
                gathered.at[place], gathered.at[place], ring_recv.at[(place + chips - hops) % chips]
            ).wait()

            @pl.when(hops < right_hops)
            def _():
                ring_copy(0, hops).start()

            @pl.when(hops <= left_hops)
            def _():
                pltpu.make_async_copy(
                    gathered.at[place], gathered.at[place], ring_recv.at[(place + hops) % chips]
                ).wait()

            @pl.when(hops < left_hops)
            def _():
                ring_copy(1, hops).start()

        slot = (place + chips + (1 - 2 * (e % 2)) * hops) % chips
        value = jnp.dot(gathered[slot], forward_ref[...], preferred_element_type=F32)
        real, imag = value[:, :samples], value[:, samples:]
        dr[...] = real
        di[...] = imag
        dsum[...] = real + imag

        def one_tile(f, inner):
            lanes = pl.ds(pl.multiple_of(f * 128, 128), 128)
            zero = jnp.zeros((2 * width, 128), F32)
            k1, k2, k3 = [zero] * shots, [zero] * shots, [zero] * shots
            for x in range(depth):
                a1 = e1[x, :, :, lanes].reshape(2 * width, 128)
                a2 = e2[x, :, :, lanes].reshape(2 * width, 128)
                a3 = e3[x, :, :, lanes].reshape(2 * width, 128)
                for s in range(shots):
                    row = pl.ds(s * depth + x, 1)
                    k1[s] = k1[s] + a1 * dsum[row, lanes]
                    k2[s] = k2[s] + a2 * dr[row, lanes]
                    k3[s] = k3[s] + a3 * di[row, lanes]
            first = lax.broadcasted_iota(jnp.int32, (2 * width, 128), 1) + f * 128 == 0
            imag_lanes = pl.ds(pl.multiple_of(samples + f * 128, 128), 128)
            for s in range(shots):
                re = jnp.where(first, k2[s], k1[s] - k3[s])
                im = jnp.where(first, k3[s], k1[s] + k2[s])
                for h in range(surfs):
                    for b in range(2):
                        low = ((h * shots + s) * 2 + b) * per_surf
                        src = b * width + h * per_surf
                        spectrum[low:low + per_surf, lanes] = re[src:src + per_surf]
                        spectrum[low:low + per_surf, imag_lanes] = im[src:src + per_surf]
            return inner

        lax.fori_loop(0, samples // 128, one_tile, 0)
        back = jnp.dot(spectrum[...].astype(BF16), inverse_ref[...], preferred_element_type=F32)
        rows = shots * 2 * per_surf
        for h in range(surfs):
            piece = back[h * rows:(h + 1) * rows].astype(BF16)
            mine = jnp.logical_and(slot == place, surf == h)

            @pl.when(mine)
            def _():
                arrived[place, surf] = piece

            @pl.when(jnp.logical_not(mine))
            def _():
                leaving[slot, h] = piece
                leave_copy(slot, h).start()

        return carry

    lax.fori_loop(0, chips, one_chunk, 0)

    first_panel, swap, base = where_ref[0:1, :], where_ref[1:2, :], where_ref[2:3, :]
    panel = first_panel + swap + core - 2 * core * swap
    target = base
    for n in range(panels):
        target = target + jnp.where(panel == n, plan_ref[n], 0)
    rows_out = data_ref.shape[0] * data_ref.shape[1]
    place_rows = jnp.where(
        lax.broadcasted_iota(jnp.int32, (rows_out, target.shape[1]), 0) == target, 1.0, 0.0
    ).astype(BF16)

    def settle(n, carry):
        slot, other = n // surfs, n % surfs

        @pl.when(n != place * surfs + surf)
        def _():
            leave_copy(slot, other).wait_send()
            pltpu.make_async_copy(
                arrived.at[slot, other], arrived.at[slot, other], leave_recv.at[slot, other]
            ).wait()

        return carry

    lax.fori_loop(0, chips * surfs, settle, 0)
    moved = arrived[...].reshape(target.shape[1], samples)
    prediction = jnp.dot(place_rows, moved, preferred_element_type=F32)
    receivers = data_ref.shape[1]
    for s in range(shots):
        out_ref[s] = data_ref[s] - scale_ref[s] * prediction[s * receivers:(s + 1) * receivers]

    for hops in range(right_hops):
        ring_copy(0, hops).wait_send()
    for hops in range(left_hops):
        ring_copy(1, hops).wait_send()
    panel_copy.wait_send()


def on_device(chips, surfs, data, positions, plan, primaries, scale):
    shots, receivers, samples = data.shape
    depth, width, _, taps = primaries.shape
    per_surf = width // surfs
    forward, inverse = fourier_matrices(samples)
    rows = shots * 2 * per_surf
    order = [
        (2 * chip_at(c, chips), b, (s * per_surf + q) * 2 * chips)
        for c in range(chips)
        for _ in range(surfs)
        for s in range(shots)
        for b in range(2)
        for q in range(per_surf)
    ]
    where_rows = np.zeros((8, len(order)), np.int32)
    where_rows[:3] = np.array(order, np.int32).T
    vmem = pl.BlockSpec(memory_space=pltpu.VMEM)
    smem = pl.BlockSpec(memory_space=pltpu.SMEM)
    sizes = (chips, surfs, shots, depth, width, samples, taps)
    return pl.pallas_call(
        functools.partial(kernel, sizes),
        out_shape=jax.ShapeDtypeStruct(data.shape, data.dtype),
        in_specs=[smem, smem] + [vmem] * 6,
        out_specs=vmem,
        scratch_shapes=[
            pltpu.VMEM((chips, shots * depth, samples), BF16),
            pltpu.VMEM((depth * width, taps), BF16),
            pltpu.VMEM((depth, 2, width, samples), F32),
            pltpu.VMEM((depth, 2, width, samples), F32),
            pltpu.VMEM((depth, 2, width, samples), F32),
            pltpu.VMEM((shots * depth, samples), F32),
            pltpu.VMEM((shots * depth, samples), F32),
            pltpu.VMEM((shots * depth, samples), F32),
            pltpu.VMEM((surfs * rows, 2 * samples), F32),
            pltpu.VMEM((chips, surfs, rows, samples), BF16),
            pltpu.VMEM((chips, surfs, rows, samples), BF16),
            pltpu.SemaphoreType.DMA((2,)),
            pltpu.SemaphoreType.DMA((2, chips)),
            pltpu.SemaphoreType.DMA((chips,)),
            pltpu.SemaphoreType.DMA((chips, surfs)),
            pltpu.SemaphoreType.DMA((chips, surfs)),
        ],
        compiler_params=pltpu.CompilerParams(collective_id=0, has_side_effects=True),
        name="predict",
    )(
        plan,
        scale,
        jnp.asarray(where_rows),
        positions.reshape(1, receivers),
        data,
        primaries.reshape(depth * width, taps),
        jnp.asarray(forward),
        jnp.asarray(inverse),
    )


def solution(mesh):
    chips, surfs = mesh.shape["shot"] // 2, mesh.shape["surf"]
    in_specs = (P("shot", "surf", None), P("surf"), P(), P("surf", None, "shot", None), P("shot"))
    out_specs = P("shot", "surf", None)
    return jax.shard_map(
        functools.partial(on_device, chips, surfs),
        mesh=mesh, in_specs=in_specs, out_specs=out_specs, check_vma=False,
    )
```

```python
import functools
import math

import jax
import jax.numpy as jnp
import ml_dtypes
import numpy as np
from jax import lax
from jax.experimental import pallas as pl
from jax.experimental.pallas import tpu as pltpu
from jax.sharding import PartitionSpec as P

MESH = pl.DeviceIdType.MESH
F32 = jnp.float32
BF16 = jnp.bfloat16
UNROLL = 8


def fourier_matrices(samples):
    length = 2 * samples
    index = np.arange(samples)
    angles = (index[:, None] * index[None, :] % length) * (2.0 * math.pi / length)
    cosine, sine = np.cos(angles), np.sin(angles)
    alternate = 1.0 - 2.0 * (index % 2)
    forward_imag = -sine
    forward_imag[:, 0] = alternate
    forward = np.concatenate([cosine, forward_imag], axis=1)
    weights = np.where(index == 0, 1.0, 2.0) / length
    weights = np.concatenate([weights, weights])
    inverse = forward.T * weights[:, None]
    return forward.astype(ml_dtypes.bfloat16), inverse.astype(ml_dtypes.bfloat16)


def chip_at(place, chips):
    half = chips // 2
    side = place // half
    return 2 * (place + side * (chips - 1 - 2 * place)) + side


def kernel(
    sizes,
    plan_ref, scale_ref, where_ref, positions_ref, data_ref, primaries_ref, forward_ref, inverse_ref,
    out_ref,
    gathered, partner, e1, e2, e3, factors, spectrum, leaving, arrived,
    panel_sems, ring_send, ring_recv, leave_send, leave_recv,
):
    chips, surfs, shots, depth, width, samples, taps = sizes
    per_surf = width // surfs
    panels = 2 * chips
    shot = lax.axis_index("shot")
    surf = lax.axis_index("surf")
    chip, core = shot // 2, shot % 2
    height, side = chip // 2, chip % 2
    place = height + side * (chips - 1 - 2 * height)
    right = chip_at((place + 1) % chips, chips) * 2 + core
    left = chip_at((place + chips - 1) % chips, chips) * 2 + core

    barrier = pltpu.get_barrier_semaphore()
    pl.semaphore_signal(barrier, inc=1, device_id=(chip * 2 + 1 - core, surf), device_id_type=MESH)

    def greet(n, carry):
        other = (n // surfs) * 2 + core
        to = n % surfs

        @pl.when(n != chip * surfs + surf)
        def _():
            pl.semaphore_signal(barrier, inc=1, device_id=(other, to), device_id_type=MESH)

        return carry

    lax.fori_loop(0, chips * surfs, greet, 0)

    local = positions_ref[...] - surf * depth
    onehot = jnp.where(
        lax.broadcasted_iota(jnp.int32, (depth, local.shape[1]), 0) == local, 1.0, 0.0
    ).astype(BF16)
    for s in range(shots):
        value = data_ref[s]
        top = value.astype(BF16)
        rest = value - top.astype(F32)
        middle = rest.astype(BF16)
        low = (rest - middle.astype(F32)).astype(BF16)
        total = (
            jnp.dot(onehot, top, preferred_element_type=F32)
            + jnp.dot(onehot, middle, preferred_element_type=F32)
            + jnp.dot(onehot, low, preferred_element_type=F32)
        )
        gathered[place, s * depth:(s + 1) * depth, :] = total.astype(BF16)

    pl.semaphore_wait(barrier, chips * surfs)

    def ring_copy(direction, hops):
        if direction == 0:
            slot, to = (place + chips - hops) % chips, right
        else:
            slot, to = (place + hops) % chips, left
        return pltpu.make_async_remote_copy(
            src_ref=gathered.at[slot],
            dst_ref=gathered.at[slot],
            send_sem=ring_send.at[direction, hops],
            recv_sem=ring_recv.at[slot],
            device_id=(to, surf),
            device_id_type=MESH,
        )

    right_hops, left_hops = chips // 2, (chips - 1) // 2
    ring_copy(0, 0).start()
    ring_copy(1, 0).start()
    panel_copy = pltpu.make_async_remote_copy(
        src_ref=primaries_ref,
        dst_ref=partner,
        send_sem=panel_sems.at[0],
        recv_sem=panel_sems.at[1],
        device_id=(chip * 2 + 1 - core, surf),
        device_id_type=MESH,
    )
    panel_copy.start()

    block = 8

    def panel_spectra(source, which):
        def step(n, carry):
            rows = source[pl.ds(pl.multiple_of(n * block * width, block * width), block * width), :]
            value = jnp.dot(rows, forward_ref[:taps, :], preferred_element_type=F32)
            real, imag = value[:, :samples], value[:, samples:]
            first = lax.broadcasted_iota(jnp.int32, real.shape, 1) == 0
            shape = (block, width, 128)
            at = pl.ds(n * block, block)
            values = (
                jnp.where(first, 0.0, real),
                jnp.where(first, real, imag - real),
                jnp.where(first, imag, imag + real),
            )
            for ref, value in zip((e1, e2, e3), values):
                for f in range(samples // 128):
                    ref[f, at, which] = value[:, f * 128:(f + 1) * 128].reshape(shape)
            return carry

        lax.fori_loop(0, depth // block, step, 0)

    panel_spectra(primaries_ref, 0)
    panel_copy.wait_recv()
    panel_spectra(partner, 1)

    def leave_copy(slot, to):
        return pltpu.make_async_remote_copy(
            src_ref=leaving.at[slot, to],
            dst_ref=arrived.at[place, surf],
            send_sem=leave_send.at[slot, to],
            recv_sem=leave_recv.at[place, surf],
            device_id=(chip_at(slot, chips) * 2 + core, to),
            device_id_type=MESH,
        )

    def one_chunk(e, carry):
        hops = (e + 1) // 2

        @pl.when(e % 2 == 1)
        def _():
            pltpu.make_async_copy(
                gathered.at[place], gathered.at[place], ring_recv.at[(place + chips - hops) % chips]
            ).wait()

            @pl.when(hops < right_hops)
            def _():
                ring_copy(0, hops).start()

            @pl.when(hops <= left_hops)
            def _():
                pltpu.make_async_copy(
                    gathered.at[place], gathered.at[place], ring_recv.at[(place + hops) % chips]
                ).wait()

            @pl.when(hops < left_hops)
            def _():
                ring_copy(1, hops).start()

        slot = (place + chips + (1 - 2 * (e % 2)) * hops) % chips
        value = jnp.dot(gathered[slot], forward_ref[...], preferred_element_type=F32)
        real, imag = value[:, :samples], value[:, samples:]
        for k, part in enumerate((real + imag, real, imag)):
            for s in range(shots):
                for f in range(samples // 128):
                    factors[f, s * 3 + k, :depth, :] = part[
                        s * depth:(s + 1) * depth, f * 128:(f + 1) * 128
                    ]

        def one_tile(f, inner):
            lanes = pl.ds(pl.multiple_of(f * 128, 128), 128)
            tiles = 2 * width // 8

            def positions(n, sums):
                sums = list(sums)
                for j in range(UNROLL):
                    x = n * UNROLL + j
                    rows = [
                        [
                            jnp.broadcast_to(
                                factors.at[f, s * 3 + k, pl.ds(pl.multiple_of(n * UNROLL, UNROLL), UNROLL)][j:j + 1],
                                (8, 128),
                            )
                            for k in range(3)
                        ]
                        for s in range(shots)
                    ]
                    for t in range(tiles):
                        b, q = t * 8 // width, t * 8 % width
                        for k, ref in enumerate((e1, e2, e3)):
                            factor = ref[f, x, b, q:q + 8]
                            for s in range(shots):
                                at = (s * 3 + k) * tiles + t
                                sums[at] = sums[at] + factor * rows[s][k]
                return tuple(sums)

            zero = jnp.zeros((8, 128), F32)
            sums = lax.fori_loop(
                0, depth // UNROLL, positions, (zero,) * (3 * shots * tiles)
            )
            k1, k2, k3 = [
                [
                    jnp.concatenate(sums[(s * 3 + k) * tiles:(s * 3 + k + 1) * tiles], axis=0)
                    for s in range(shots)
                ]
                for k in range(3)
            ]
            first = lax.broadcasted_iota(jnp.int32, (2 * width, 128), 1) + f * 128 == 0
            imag_lanes = pl.ds(pl.multiple_of(samples + f * 128, 128), 128)
            for s in range(shots):
                re = jnp.where(first, k2[s], k1[s] - k3[s])
                im = jnp.where(first, k3[s], k1[s] + k2[s])
                for h in range(surfs):
                    for b in range(2):
                        low = ((h * shots + s) * 2 + b) * per_surf
                        src = b * width + h * per_surf
                        spectrum[low:low + per_surf, lanes] = re[src:src + per_surf]
                        spectrum[low:low + per_surf, imag_lanes] = im[src:src + per_surf]
            return inner

        lax.fori_loop(0, samples // 128, one_tile, 0)
        back = jnp.dot(spectrum[...].astype(BF16), inverse_ref[...], preferred_element_type=F32)
        rows = shots * 2 * per_surf
        for h in range(surfs):
            piece = back[h * rows:(h + 1) * rows].astype(BF16)
            mine = jnp.logical_and(slot == place, surf == h)

            @pl.when(mine)
            def _():
                arrived[place, surf] = piece

            @pl.when(jnp.logical_not(mine))
            def _():
                leaving[slot, h] = piece
                leave_copy(slot, h).start()

        return carry

    lax.fori_loop(0, chips, one_chunk, 0)

    first_panel, swap, base = where_ref[0:1, :], where_ref[1:2, :], where_ref[2:3, :]
    panel = first_panel + swap + core - 2 * core * swap
    target = base
    for n in range(panels):
        target = target + jnp.where(panel == n, plan_ref[n], 0)
    rows_out = data_ref.shape[0] * data_ref.shape[1]
    place_rows = jnp.where(
        lax.broadcasted_iota(jnp.int32, (rows_out, target.shape[1]), 0) == target, 1.0, 0.0
    ).astype(BF16)

    def settle(n, carry):
        slot, other = n // surfs, n % surfs

        @pl.when(n != place * surfs + surf)
        def _():
            leave_copy(slot, other).wait_send()
            pltpu.make_async_copy(
                arrived.at[slot, other], arrived.at[slot, other], leave_recv.at[slot, other]
            ).wait()

        return carry

    lax.fori_loop(0, chips * surfs, settle, 0)
    moved = arrived[...].reshape(target.shape[1], samples)
    prediction = jnp.dot(place_rows, moved, preferred_element_type=F32)
    receivers = data_ref.shape[1]
    for s in range(shots):
        out_ref[s] = data_ref[s] - scale_ref[s] * prediction[s * receivers:(s + 1) * receivers]

    for hops in range(right_hops):
        ring_copy(0, hops).wait_send()
    for hops in range(left_hops):
        ring_copy(1, hops).wait_send()
    panel_copy.wait_send()


def on_device(chips, surfs, data, positions, plan, primaries, scale):
    shots, receivers, samples = data.shape
    depth, width, _, taps = primaries.shape
    per_surf = width // surfs
    forward, inverse = fourier_matrices(samples)
    rows = shots * 2 * per_surf
    order = [
        (2 * chip_at(c, chips), b, (s * per_surf + q) * 2 * chips)
        for c in range(chips)
        for _ in range(surfs)
        for s in range(shots)
        for b in range(2)
        for q in range(per_surf)
    ]
    where_rows = np.zeros((8, len(order)), np.int32)
    where_rows[:3] = np.array(order, np.int32).T
    vmem = pl.BlockSpec(memory_space=pltpu.VMEM)
    smem = pl.BlockSpec(memory_space=pltpu.SMEM)
    sizes = (chips, surfs, shots, depth, width, samples, taps)
    return pl.pallas_call(
        functools.partial(kernel, sizes),
        out_shape=jax.ShapeDtypeStruct(data.shape, data.dtype),
        in_specs=[smem, smem] + [vmem] * 6,
        out_specs=vmem,
        scratch_shapes=[
            pltpu.VMEM((chips, shots * depth, samples), BF16),
            pltpu.VMEM((depth * width, taps), BF16),
            pltpu.VMEM((samples // 128, depth, 2, width, 128), F32),
            pltpu.VMEM((samples // 128, depth, 2, width, 128), F32),
            pltpu.VMEM((samples // 128, depth, 2, width, 128), F32),
            pltpu.VMEM((samples // 128, shots * 3, depth + 8, 128), F32),
            pltpu.VMEM((surfs * rows, 2 * samples), F32),
            pltpu.VMEM((chips, surfs, rows, samples), BF16),
            pltpu.VMEM((chips, surfs, rows, samples), BF16),
            pltpu.SemaphoreType.DMA((2,)),
            pltpu.SemaphoreType.DMA((2, chips)),
            pltpu.SemaphoreType.DMA((chips,)),
            pltpu.SemaphoreType.DMA((chips, surfs)),
            pltpu.SemaphoreType.DMA((chips, surfs)),
        ],
        compiler_params=pltpu.CompilerParams(collective_id=0, has_side_effects=True),
        name="predict",
    )(
        plan,
        scale,
        jnp.asarray(where_rows),
        positions.reshape(1, receivers),
        data,
        primaries.reshape(depth * width, taps),
        jnp.asarray(forward),
        jnp.asarray(inverse),
    )


def solution(mesh):
    chips, surfs = mesh.shape["shot"] // 2, mesh.shape["surf"]
    in_specs = (P("shot", "surf", None), P("surf"), P(), P("surf", None, "shot", None), P("shot"))
    out_specs = P("shot", "surf", None)
    return jax.shard_map(
        functools.partial(on_device, chips, surfs),
        mesh=mesh, in_specs=in_specs, out_specs=out_specs, check_vma=False,
    )
```

```python
import functools
import math

import jax
import jax.numpy as jnp
import ml_dtypes
import numpy as np
from jax import lax
from jax.experimental import pallas as pl
from jax.experimental.pallas import tpu as pltpu
from jax.sharding import PartitionSpec as P

MESH = pl.DeviceIdType.MESH
F32 = jnp.float32
BF16 = jnp.bfloat16
UNROLL = 16


def fourier_matrices(samples):
    length = 2 * samples
    index = np.arange(samples)
    angles = (index[:, None] * index[None, :] % length) * (2.0 * math.pi / length)
    cosine, sine = np.cos(angles), np.sin(angles)
    alternate = 1.0 - 2.0 * (index % 2)
    forward_imag = -sine
    forward_imag[:, 0] = alternate
    forward = np.concatenate([cosine, forward_imag], axis=1)
    weights = np.where(index == 0, 1.0, 2.0) / length
    weights = np.concatenate([weights, weights])
    inverse = forward.T * weights[:, None]
    return forward.astype(ml_dtypes.bfloat16), inverse.astype(ml_dtypes.bfloat16)


def chip_at(place, chips):
    half = chips // 2
    side = place // half
    return 2 * (place + side * (chips - 1 - 2 * place)) + side


def kernel(
    sizes,
    plan_ref, scale_ref, where_ref, positions_ref, data_ref, primaries_ref, forward_hbm, inverse_hbm,
    out_ref,
    forward_ref, inverse_ref, gathered, partner, e1, e2, e3, factors, spectrum,
    crossing, crossed, leaving, arrived,
    load_sems, panel_sems, ring_send, ring_recv, cross_send, cross_recv, leave_send, leave_recv,
):
    chips, surfs, shots, depth, width, samples, taps = sizes
    per_surf = width // surfs
    panels = 2 * chips
    shot = lax.axis_index("shot")
    surf = lax.axis_index("surf")
    chip, core = shot // 2, shot % 2
    height, side = chip // 2, chip % 2
    place = height + side * (chips - 1 - 2 * height)
    right = chip_at((place + 1) % chips, chips) * 2 + core
    left = chip_at((place + chips - 1) % chips, chips) * 2 + core

    barrier = pltpu.get_barrier_semaphore()
    pl.semaphore_signal(barrier, inc=1, device_id=(chip * 2 + 1 - core, surf), device_id_type=MESH)

    for to in (right, left):
        pl.semaphore_signal(barrier, inc=1, device_id=(to, surf), device_id_type=MESH)
    for h in range(surfs):

        @pl.when(h != surf)
        def _():
            pl.semaphore_signal(barrier, inc=1, device_id=(shot, h), device_id_type=MESH)

    load_forward = pltpu.make_async_copy(forward_hbm, forward_ref, load_sems.at[0])
    load_inverse = pltpu.make_async_copy(inverse_hbm, inverse_ref, load_sems.at[1])
    load_forward.start()
    load_inverse.start()

    local = positions_ref[...] - surf * depth
    onehot = jnp.where(
        lax.broadcasted_iota(jnp.int32, (depth, local.shape[1]), 0) == local, 1.0, 0.0
    ).astype(BF16)
    for s in range(shots):
        value = data_ref[s]
        top = value.astype(BF16)
        rest = value - top.astype(F32)
        middle = rest.astype(BF16)
        low = (rest - middle.astype(F32)).astype(BF16)
        total = (
            jnp.dot(onehot, top, preferred_element_type=F32)
            + jnp.dot(onehot, middle, preferred_element_type=F32)
            + jnp.dot(onehot, low, preferred_element_type=F32)
        )
        gathered[place, s * depth:(s + 1) * depth, :] = total.astype(BF16)

    pl.semaphore_wait(barrier, surfs + 2)

    def ring_copy(direction, hops):
        if direction == 0:
            slot, to = (place + chips - hops) % chips, right
        else:
            slot, to = (place + hops) % chips, left
        return pltpu.make_async_remote_copy(
            src_ref=gathered.at[slot],
            dst_ref=gathered.at[slot],
            send_sem=ring_send.at[direction, hops],
            recv_sem=ring_recv.at[slot],
            device_id=(to, surf),
            device_id_type=MESH,
        )

    right_hops, left_hops = chips // 2, (chips - 1) // 2
    ring_copy(0, 0).start()
    ring_copy(1, 0).start()
    panel_copy = pltpu.make_async_remote_copy(
        src_ref=primaries_ref,
        dst_ref=partner,
        send_sem=panel_sems.at[0],
        recv_sem=panel_sems.at[1],
        device_id=(chip * 2 + 1 - core, surf),
        device_id_type=MESH,
    )
    panel_copy.start()

    block = 8

    def panel_spectra(source, which):
        def step(n, carry):
            rows = source[pl.ds(pl.multiple_of(n * block * width, block * width), block * width), :]
            value = jnp.dot(rows, forward_ref[:taps, :], preferred_element_type=F32)
            real, imag = value[:, :samples], value[:, samples:]
            first = lax.broadcasted_iota(jnp.int32, real.shape, 1) == 0
            shape = (block, width, 128)
            at = pl.ds(n * block, block)
            values = (
                jnp.where(first, 0.0, real),
                jnp.where(first, real, imag - real),
                jnp.where(first, imag, imag + real),
            )
            for ref, value in zip((e1, e2, e3), values):
                for f in range(samples // 128):
                    ref[f, at, which] = value[:, f * 128:(f + 1) * 128].reshape(shape)
            return carry

        lax.fori_loop(0, depth // block, step, 0)

    load_forward.wait()
    panel_spectra(primaries_ref, 0)
    panel_copy.wait_recv()
    panel_spectra(partner, 1)
    load_inverse.wait()

    def cross_copy(e, to):
        return pltpu.make_async_remote_copy(
            src_ref=crossing.at[e, to],
            dst_ref=crossed.at[e, surf],
            send_sem=cross_send.at[e, to],
            recv_sem=cross_recv.at[e, surf],
            device_id=(shot, to),
            device_id_type=MESH,
        )

    def leave_copy(slot):
        return pltpu.make_async_remote_copy(
            src_ref=leaving.at[slot],
            dst_ref=arrived.at[place],
            send_sem=leave_send.at[slot],
            recv_sem=leave_recv.at[place],
            device_id=(chip_at(slot, chips) * 2 + core, surf),
            device_id_type=MESH,
        )

    def slot_of(e):
        turn = (e + 1) % chips
        hops = (turn + 1) // 2
        return (place + chips + (1 - 2 * (turn % 2)) * hops) % chips

    def combined(e):
        for h in range(surfs):

            @pl.when(h != surf)
            def _():
                pltpu.make_async_copy(crossed.at[e, h], crossed.at[e, h], cross_recv.at[e, h]).wait()

        total = crossed[e, 0].astype(F32)
        for h in range(1, surfs):
            total = total + crossed[e, h].astype(F32)
        return total.astype(BF16)

    def one_chunk(e, carry):
        turn = (e + 1) % chips
        hops = (turn + 1) // 2

        @pl.when(turn % 2 == 1)
        def _():
            pltpu.make_async_copy(
                gathered.at[place], gathered.at[place], ring_recv.at[(place + chips - hops) % chips]
            ).wait()

            @pl.when(hops < right_hops)
            def _():
                ring_copy(0, hops).start()

            @pl.when(hops <= left_hops)
            def _():
                pltpu.make_async_copy(
                    gathered.at[place], gathered.at[place], ring_recv.at[(place + hops) % chips]
                ).wait()

            @pl.when(hops < left_hops)
            def _():
                ring_copy(1, hops).start()

        slot = slot_of(e)
        value = jnp.dot(gathered[slot], forward_ref[...], preferred_element_type=F32)
        real, imag = value[:, :samples], value[:, samples:]
        for k, part in enumerate((real + imag, real, imag)):
            for s in range(shots):
                for f in range(samples // 128):
                    factors[f, s * 3 + k, :depth, :] = part[
                        s * depth:(s + 1) * depth, f * 128:(f + 1) * 128
                    ]

        def one_tile(f, inner):
            lanes = pl.ds(pl.multiple_of(f * 128, 128), 128)
            tiles = 2 * width // 8

            def positions(n, sums):
                sums = list(sums)
                for j in range(UNROLL):
                    x = n * UNROLL + j
                    rows = [
                        [
                            jnp.broadcast_to(
                                factors.at[f, s * 3 + k, pl.ds(pl.multiple_of(n * UNROLL, UNROLL), UNROLL)][j:j + 1],
                                (8, 128),
                            )
                            for k in range(3)
                        ]
                        for s in range(shots)
                    ]
                    for t in range(tiles):
                        b, q = t * 8 // width, t * 8 % width
                        for k, ref in enumerate((e1, e2, e3)):
                            factor = ref[f, x, b, q:q + 8]
                            for s in range(shots):
                                at = (s * 3 + k) * tiles + t
                                sums[at] = sums[at] + factor * rows[s][k]
                return tuple(sums)

            zero = jnp.zeros((8, 128), F32)
            sums = lax.fori_loop(
                0, depth // UNROLL, positions, (zero,) * (3 * shots * tiles)
            )
            k1, k2, k3 = [
                [
                    jnp.concatenate(sums[(s * 3 + k) * tiles:(s * 3 + k + 1) * tiles], axis=0)
                    for s in range(shots)
                ]
                for k in range(3)
            ]
            first = lax.broadcasted_iota(jnp.int32, (2 * width, 128), 1) + f * 128 == 0
            imag_lanes = pl.ds(pl.multiple_of(samples + f * 128, 128), 128)
            for s in range(shots):
                re = jnp.where(first, k2[s], k1[s] - k3[s])
                im = jnp.where(first, k3[s], k1[s] + k2[s])
                for h in range(surfs):
                    for b in range(2):
                        low = ((h * shots + s) * 2 + b) * per_surf
                        src = b * width + h * per_surf
                        spectrum[low:low + per_surf, lanes] = re[src:src + per_surf]
                        spectrum[low:low + per_surf, imag_lanes] = im[src:src + per_surf]
            return inner

        lax.fori_loop(0, samples // 128, one_tile, 0)
        back = jnp.dot(spectrum[...].astype(BF16), inverse_ref[...], preferred_element_type=F32)
        rows = shots * 2 * per_surf
        for h in range(surfs):
            piece = back[h * rows:(h + 1) * rows].astype(BF16)

            @pl.when(surf == h)
            def _():
                crossed[e, h] = piece

            @pl.when(surf != h)
            def _():
                crossing[e, h] = piece
                cross_copy(e, h).start()

        @pl.when(e > 0)
        def _():
            before = slot_of(e - 1)
            leaving[before] = combined(e - 1)
            leave_copy(before).start()

        return carry

    lax.fori_loop(0, chips, one_chunk, 0)
    arrived[place] = combined(chips - 1)

    first_panel, swap, base = where_ref[0:1, :], where_ref[1:2, :], where_ref[2:3, :]
    panel = first_panel + swap + core - 2 * core * swap
    target = base
    for n in range(panels):
        target = target + jnp.where(panel == n, plan_ref[n], 0)
    rows_out = data_ref.shape[0] * data_ref.shape[1]
    place_rows = jnp.where(
        lax.broadcasted_iota(jnp.int32, (rows_out, target.shape[1]), 0) == target, 1.0, 0.0
    ).astype(BF16)

    def settle(n, carry):
        for h in range(surfs):

            @pl.when(h != surf)
            def _():
                cross_copy(n, h).wait_send()

        @pl.when(n != place)
        def _():
            leave_copy(n).wait_send()
            pltpu.make_async_copy(arrived.at[n], arrived.at[n], leave_recv.at[n]).wait()

        return carry

    lax.fori_loop(0, chips, settle, 0)
    moved = arrived[...].reshape(target.shape[1], samples)
    prediction = jnp.dot(place_rows, moved, preferred_element_type=F32)
    receivers = data_ref.shape[1]
    for s in range(shots):
        out_ref[s] = data_ref[s] - scale_ref[s] * prediction[s * receivers:(s + 1) * receivers]

    for hops in range(right_hops):
        ring_copy(0, hops).wait_send()
    for hops in range(left_hops):
        ring_copy(1, hops).wait_send()
    panel_copy.wait_send()


def on_device(chips, surfs, data, positions, plan, primaries, scale):
    shots, receivers, samples = data.shape
    depth, width, _, taps = primaries.shape
    per_surf = width // surfs
    forward, inverse = fourier_matrices(samples)
    rows = shots * 2 * per_surf
    order = [
        (2 * chip_at(c, chips), b, (s * per_surf + q) * 2 * chips)
        for c in range(chips)
        for s in range(shots)
        for b in range(2)
        for q in range(per_surf)
    ]
    where_rows = np.zeros((8, len(order)), np.int32)
    where_rows[:3] = np.array(order, np.int32).T
    vmem = pl.BlockSpec(memory_space=pltpu.VMEM)
    smem = pl.BlockSpec(memory_space=pltpu.SMEM)
    sizes = (chips, surfs, shots, depth, width, samples, taps)
    return pl.pallas_call(
        functools.partial(kernel, sizes),
        out_shape=jax.ShapeDtypeStruct(data.shape, data.dtype),
        in_specs=[smem, smem] + [vmem] * 4 + [pl.BlockSpec(memory_space=pl.ANY)] * 2,
        out_specs=vmem,
        scratch_shapes=[
            pltpu.VMEM(forward.shape, BF16),
            pltpu.VMEM(inverse.shape, BF16),
            pltpu.VMEM((chips, shots * depth, samples), BF16),
            pltpu.VMEM((depth * width, taps), BF16),
            pltpu.VMEM((samples // 128, depth, 2, width, 128), F32),
            pltpu.VMEM((samples // 128, depth, 2, width, 128), F32),
            pltpu.VMEM((samples // 128, depth, 2, width, 128), F32),
            pltpu.VMEM((samples // 128, shots * 3, depth + 8, 128), F32),
            pltpu.VMEM((surfs * rows, 2 * samples), F32),
            pltpu.VMEM((chips, surfs, rows, samples), BF16),
            pltpu.VMEM((chips, surfs, rows, samples), BF16),
            pltpu.VMEM((chips, rows, samples), BF16),
            pltpu.VMEM((chips, rows, samples), BF16),
            pltpu.SemaphoreType.DMA((2,)),
            pltpu.SemaphoreType.DMA((2,)),
            pltpu.SemaphoreType.DMA((2, chips)),
            pltpu.SemaphoreType.DMA((chips,)),
            pltpu.SemaphoreType.DMA((chips, surfs)),
            pltpu.SemaphoreType.DMA((chips, surfs)),
            pltpu.SemaphoreType.DMA((chips,)),
            pltpu.SemaphoreType.DMA((chips,)),
        ],
        compiler_params=pltpu.CompilerParams(collective_id=0, has_side_effects=True),
        name="predict",
    )(
        plan,
        scale,
        jnp.asarray(where_rows),
        positions.reshape(1, receivers),
        data,
        primaries.reshape(depth * width, taps),
        jnp.asarray(forward),
        jnp.asarray(inverse),
    )


def solution(mesh):
    chips, surfs = mesh.shape["shot"] // 2, mesh.shape["surf"]
    in_specs = (P("shot", "surf", None), P("surf"), P(), P("surf", None, "shot", None), P("shot"))
    out_specs = P("shot", "surf", None)
    return jax.shard_map(
        functools.partial(on_device, chips, surfs),
        mesh=mesh, in_specs=in_specs, out_specs=out_specs, check_vma=False,
    )
```

```python
import functools
import math

import jax
import jax.numpy as jnp
import ml_dtypes
import numpy as np
from jax import lax
from jax.experimental import pallas as pl
from jax.experimental.pallas import tpu as pltpu
from jax.sharding import PartitionSpec as P

MESH = pl.DeviceIdType.MESH
F32 = jnp.float32
BF16 = jnp.bfloat16
UNROLL = 16
LAG = 2


def fourier_matrices(samples):
    length = 2 * samples
    index = np.arange(samples)
    angles = (index[:, None] * index[None, :] % length) * (2.0 * math.pi / length)
    cosine, sine = np.cos(angles), np.sin(angles)
    alternate = 1.0 - 2.0 * (index % 2)
    forward_imag = -sine
    forward_imag[:, 0] = alternate
    forward = np.concatenate([cosine, forward_imag], axis=1)
    weights = np.where(index == 0, 1.0, 2.0) / length
    weights = np.concatenate([weights, weights])
    inverse = forward.T * weights[:, None]
    return forward.astype(ml_dtypes.bfloat16), inverse.astype(ml_dtypes.bfloat16)


def chip_at(place, chips):
    half = chips // 2
    side = place // half
    return 2 * (place + side * (chips - 1 - 2 * place)) + side


def kernel(
    sizes,
    plan_ref, scale_ref, where_ref, positions_ref, data_ref, primaries_ref, forward_hbm, inverse_hbm,
    out_ref,
    forward_ref, inverse_ref, gathered, partner, e1, e2, e3, factors, spectrum,
    crossing, crossed, leaving, arrived,
    load_sems, panel_sems, ring_send, ring_recv, cross_send, cross_recv, leave_send, leave_recv,
):
    chips, surfs, shots, depth, width, samples, taps = sizes
    per_surf = width // surfs
    panels = 2 * chips
    shot = lax.axis_index("shot")
    surf = lax.axis_index("surf")
    chip, core = shot // 2, shot % 2
    height, side = chip // 2, chip % 2
    place = height + side * (chips - 1 - 2 * height)
    right = chip_at((place + 1) % chips, chips) * 2 + core
    left = chip_at((place + chips - 1) % chips, chips) * 2 + core

    barrier = pltpu.get_barrier_semaphore()
    pl.semaphore_signal(barrier, inc=1, device_id=(chip * 2 + 1 - core, surf), device_id_type=MESH)

    for to in (right, left):
        pl.semaphore_signal(barrier, inc=1, device_id=(to, surf), device_id_type=MESH)
    for h in range(surfs):

        @pl.when(h != surf)
        def _():
            pl.semaphore_signal(barrier, inc=1, device_id=(shot, h), device_id_type=MESH)

    load_forward = pltpu.make_async_copy(forward_hbm, forward_ref, load_sems.at[0])
    load_inverse = pltpu.make_async_copy(inverse_hbm, inverse_ref, load_sems.at[1])
    load_forward.start()
    load_inverse.start()

    local = positions_ref[...] - surf * depth
    onehot = jnp.where(
        lax.broadcasted_iota(jnp.int32, (depth, local.shape[1]), 0) == local, 1.0, 0.0
    ).astype(BF16)
    for s in range(shots):
        value = data_ref[s]
        top = value.astype(BF16)
        rest = value - top.astype(F32)
        middle = rest.astype(BF16)
        low = (rest - middle.astype(F32)).astype(BF16)
        total = (
            jnp.dot(onehot, top, preferred_element_type=F32)
            + jnp.dot(onehot, middle, preferred_element_type=F32)
            + jnp.dot(onehot, low, preferred_element_type=F32)
        )
        gathered[place, s * depth:(s + 1) * depth, :] = total.astype(BF16)

    pl.semaphore_wait(barrier, surfs + 2)

    def ring_copy(direction, hops):
        if direction == 0:
            slot, to = (place + chips - hops) % chips, right
        else:
            slot, to = (place + hops) % chips, left
        return pltpu.make_async_remote_copy(
            src_ref=gathered.at[slot],
            dst_ref=gathered.at[slot],
            send_sem=ring_send.at[direction, hops],
            recv_sem=ring_recv.at[slot],
            device_id=(to, surf),
            device_id_type=MESH,
        )

    right_hops, left_hops = chips // 2, (chips - 1) // 2
    ring_copy(0, 0).start()
    ring_copy(1, 0).start()
    panel_copy = pltpu.make_async_remote_copy(
        src_ref=primaries_ref,
        dst_ref=partner,
        send_sem=panel_sems.at[0],
        recv_sem=panel_sems.at[1],
        device_id=(chip * 2 + 1 - core, surf),
        device_id_type=MESH,
    )
    panel_copy.start()

    block = 8

    def panel_spectra(source, which):
        def step(n, carry):
            rows = source[pl.ds(pl.multiple_of(n * block * width, block * width), block * width), :]
            value = jnp.dot(rows, forward_ref[:taps, :], preferred_element_type=F32)
            real, imag = value[:, :samples], value[:, samples:]
            first = lax.broadcasted_iota(jnp.int32, real.shape, 1) == 0
            shape = (block, width, 128)
            at = pl.ds(n * block, block)
            values = (
                jnp.where(first, 0.0, real),
                jnp.where(first, real, imag - real),
                jnp.where(first, imag, imag + real),
            )
            for ref, value in zip((e1, e2, e3), values):
                for f in range(samples // 128):
                    ref[f, at, which] = value[:, f * 128:(f + 1) * 128].reshape(shape)
            return carry

        lax.fori_loop(0, depth // block, step, 0)

    load_forward.wait()
    panel_spectra(primaries_ref, 0)
    panel_copy.wait_recv()
    panel_spectra(partner, 1)
    load_inverse.wait()

    def cross_copy(e, to):
        return pltpu.make_async_remote_copy(
            src_ref=crossing.at[e, to],
            dst_ref=crossed.at[e, surf],
            send_sem=cross_send.at[e, to],
            recv_sem=cross_recv.at[e, surf],
            device_id=(shot, to),
            device_id_type=MESH,
        )

    def leave_copy(slot):
        return pltpu.make_async_remote_copy(
            src_ref=leaving.at[slot],
            dst_ref=arrived.at[place],
            send_sem=leave_send.at[slot],
            recv_sem=leave_recv.at[place],
            device_id=(chip_at(slot, chips) * 2 + core, surf),
            device_id_type=MESH,
        )

    def slot_of(e):
        turn = (e + 1) % chips
        hops = (turn + 1) // 2
        return (place + chips + (1 - 2 * (turn % 2)) * hops) % chips

    def combined(e):
        for h in range(surfs):

            @pl.when(h != surf)
            def _():
                pltpu.make_async_copy(crossed.at[e, h], crossed.at[e, h], cross_recv.at[e, h]).wait()

        total = crossed[e, 0].astype(F32)
        for h in range(1, surfs):
            total = total + crossed[e, h].astype(F32)
        return total.astype(BF16)

    def pass_on(e):
        slot = slot_of(e)
        leaving[slot] = combined(e)
        leave_copy(slot).start()

    def one_chunk(e, carry):
        turn = (e + 1) % chips
        hops = (turn + 1) // 2

        @pl.when(turn % 2 == 1)
        def _():
            pltpu.make_async_copy(
                gathered.at[place], gathered.at[place], ring_recv.at[(place + chips - hops) % chips]
            ).wait()

            @pl.when(hops < right_hops)
            def _():
                ring_copy(0, hops).start()

            @pl.when(hops <= left_hops)
            def _():
                pltpu.make_async_copy(
                    gathered.at[place], gathered.at[place], ring_recv.at[(place + hops) % chips]
                ).wait()

            @pl.when(hops < left_hops)
            def _():
                ring_copy(1, hops).start()

        slot = slot_of(e)
        value = jnp.dot(gathered[slot], forward_ref[...], preferred_element_type=F32)
        real, imag = value[:, :samples], value[:, samples:]
        for k, part in enumerate((real + imag, real, imag)):
            for s in range(shots):
                for f in range(samples // 128):
                    factors[f, s * 3 + k, :depth, :] = part[
                        s * depth:(s + 1) * depth, f * 128:(f + 1) * 128
                    ]

        def one_tile(f, inner):
            lanes = pl.ds(pl.multiple_of(f * 128, 128), 128)
            tiles = 2 * width // 8

            def positions(n, sums):
                sums = list(sums)
                for j in range(UNROLL):
                    x = n * UNROLL + j
                    rows = [
                        [
                            jnp.broadcast_to(
                                factors.at[f, s * 3 + k, pl.ds(pl.multiple_of(n * UNROLL, UNROLL), UNROLL)][j:j + 1],
                                (8, 128),
                            )
                            for k in range(3)
                        ]
                        for s in range(shots)
                    ]
                    for t in range(tiles):
                        b, q = t * 8 // width, t * 8 % width
                        for k, ref in enumerate((e1, e2, e3)):
                            factor = ref[f, x, b, q:q + 8]
                            for s in range(shots):
                                at = (s * 3 + k) * tiles + t
                                sums[at] = sums[at] + factor * rows[s][k]
                return tuple(sums)

            zero = jnp.zeros((8, 128), F32)
            sums = lax.fori_loop(
                0, depth // UNROLL, positions, (zero,) * (3 * shots * tiles)
            )
            k1, k2, k3 = [
                [
                    jnp.concatenate(sums[(s * 3 + k) * tiles:(s * 3 + k + 1) * tiles], axis=0)
                    for s in range(shots)
                ]
                for k in range(3)
            ]
            first = lax.broadcasted_iota(jnp.int32, (2 * width, 128), 1) + f * 128 == 0
            imag_lanes = pl.ds(pl.multiple_of(samples + f * 128, 128), 128)
            for s in range(shots):
                re = jnp.where(first, k2[s], k1[s] - k3[s])
                im = jnp.where(first, k3[s], k1[s] + k2[s])
                for h in range(surfs):
                    for b in range(2):
                        low = ((h * shots + s) * 2 + b) * per_surf
                        src = b * width + h * per_surf
                        spectrum[low:low + per_surf, lanes] = re[src:src + per_surf]
                        spectrum[low:low + per_surf, imag_lanes] = im[src:src + per_surf]
            return inner

        lax.fori_loop(0, samples // 128, one_tile, 0)
        back = jnp.dot(spectrum[...].astype(BF16), inverse_ref[...], preferred_element_type=F32)
        rows = shots * 2 * per_surf
        for h in range(surfs):
            piece = back[h * rows:(h + 1) * rows].astype(BF16)

            @pl.when(surf == h)
            def _():
                crossed[e, h] = piece

            @pl.when(surf != h)
            def _():
                crossing[e, h] = piece
                cross_copy(e, h).start()

        @pl.when(e >= LAG)
        def _():
            pass_on(e - LAG)

        return carry

    lax.fori_loop(0, chips, one_chunk, 0)
    for e in range(chips - LAG, chips - 1):
        pass_on(e)
    arrived[place] = combined(chips - 1)

    first_panel, swap, base = where_ref[0:1, :], where_ref[1:2, :], where_ref[2:3, :]
    panel = first_panel + swap + core - 2 * core * swap
    target = base
    for n in range(panels):
        target = target + jnp.where(panel == n, plan_ref[n], 0)
    rows_out = data_ref.shape[0] * data_ref.shape[1]
    place_rows = jnp.where(
        lax.broadcasted_iota(jnp.int32, (rows_out, target.shape[1]), 0) == target, 1.0, 0.0
    ).astype(BF16)

    def settle(n, carry):
        for h in range(surfs):

            @pl.when(h != surf)
            def _():
                cross_copy(n, h).wait_send()

        @pl.when(n != place)
        def _():
            leave_copy(n).wait_send()
            pltpu.make_async_copy(arrived.at[n], arrived.at[n], leave_recv.at[n]).wait()

        return carry

    lax.fori_loop(0, chips, settle, 0)
    moved = arrived[...].reshape(target.shape[1], samples)
    prediction = jnp.dot(place_rows, moved, preferred_element_type=F32)
    receivers = data_ref.shape[1]
    for s in range(shots):
        out_ref[s] = data_ref[s] - scale_ref[s] * prediction[s * receivers:(s + 1) * receivers]

    for hops in range(right_hops):
        ring_copy(0, hops).wait_send()
    for hops in range(left_hops):
        ring_copy(1, hops).wait_send()
    panel_copy.wait_send()


def on_device(chips, surfs, data, positions, plan, primaries, scale):
    shots, receivers, samples = data.shape
    depth, width, _, taps = primaries.shape
    per_surf = width // surfs
    forward, inverse = fourier_matrices(samples)
    rows = shots * 2 * per_surf
    order = [
        (2 * chip_at(c, chips), b, (s * per_surf + q) * 2 * chips)
        for c in range(chips)
        for s in range(shots)
        for b in range(2)
        for q in range(per_surf)
    ]
    where_rows = np.zeros((8, len(order)), np.int32)
    where_rows[:3] = np.array(order, np.int32).T
    vmem = pl.BlockSpec(memory_space=pltpu.VMEM)
    smem = pl.BlockSpec(memory_space=pltpu.SMEM)
    sizes = (chips, surfs, shots, depth, width, samples, taps)
    return pl.pallas_call(
        functools.partial(kernel, sizes),
        out_shape=jax.ShapeDtypeStruct(data.shape, data.dtype),
        in_specs=[smem, smem] + [vmem] * 4 + [pl.BlockSpec(memory_space=pl.ANY)] * 2,
        out_specs=vmem,
        scratch_shapes=[
            pltpu.VMEM(forward.shape, BF16),
            pltpu.VMEM(inverse.shape, BF16),
            pltpu.VMEM((chips, shots * depth, samples), BF16),
            pltpu.VMEM((depth * width, taps), BF16),
            pltpu.VMEM((samples // 128, depth, 2, width, 128), F32),
            pltpu.VMEM((samples // 128, depth, 2, width, 128), F32),
            pltpu.VMEM((samples // 128, depth, 2, width, 128), F32),
            pltpu.VMEM((samples // 128, shots * 3, depth + 8, 128), F32),
            pltpu.VMEM((surfs * rows, 2 * samples), F32),
            pltpu.VMEM((chips, surfs, rows, samples), BF16),
            pltpu.VMEM((chips, surfs, rows, samples), BF16),
            pltpu.VMEM((chips, rows, samples), BF16),
            pltpu.VMEM((chips, rows, samples), BF16),
            pltpu.SemaphoreType.DMA((2,)),
            pltpu.SemaphoreType.DMA((2,)),
            pltpu.SemaphoreType.DMA((2, chips)),
            pltpu.SemaphoreType.DMA((chips,)),
            pltpu.SemaphoreType.DMA((chips, surfs)),
            pltpu.SemaphoreType.DMA((chips, surfs)),
            pltpu.SemaphoreType.DMA((chips,)),
            pltpu.SemaphoreType.DMA((chips,)),
        ],
        compiler_params=pltpu.CompilerParams(collective_id=0, has_side_effects=True),
        name="predict",
    )(
        plan,
        scale,
        jnp.asarray(where_rows),
        positions.reshape(1, receivers),
        data,
        primaries.reshape(depth * width, taps),
        jnp.asarray(forward),
        jnp.asarray(inverse),
    )


def solution(mesh):
    chips, surfs = mesh.shape["shot"] // 2, mesh.shape["surf"]
    in_specs = (P("shot", "surf", None), P("surf"), P(), P("surf", None, "shot", None), P("shot"))
    out_specs = P("shot", "surf", None)
    return jax.shard_map(
        functools.partial(on_device, chips, surfs),
        mesh=mesh, in_specs=in_specs, out_specs=out_specs, check_vma=False,
    )
```
